32 devices in a mesh: grp: 4 (over y, core), dom: 8 (over z, x).
Axes of the slice: x: 2, y: 2, z: 4, core: 2. Of those that a mesh axis runs over, the one named last changes fastest.
Arguments:
- coarse: float32 [4096, 128], P(('grp', 'dom')), may hold values from -254 to 104
- region_map: int32 [131072], P(('grp', 'dom')), may hold values from 0 to 1023
- features: bfloat16 [32, 131072], P(None, ('grp', 'dom')), may hold values from 0 to 1
- reward_weights: float32 [32], replicated, may hold values from -1 to 1
- transitions: bfloat16 [1024, 8, 128, 128], P(('grp', 'dom')), may hold values from 4.9829483e-05 to 0.0009994507
- successors: int32 [1024, 8], P(('grp', 'dom')), may hold values from 0 to 39, as said below
- part_sizes: int32 [32], P(('grp', 'dom')), may hold values from 16 to 32, as said below
- outgoing_block_list: int32 [32, 8, 1], P(('grp', 'dom')), may hold values from 0 to 31, as said below
- destinations: int32 [128], replicated, may hold values from 0 to 131071, as said below
- anchors: bfloat16 [131072, 128], P(('grp', 'dom')), may hold values from 0.099609375 to 1
Outputs:
- values: bfloat16 [131072, 128], P(('grp', 'dom'))
- visits: bfloat16 [131072, 128], P(('grp', 'dom'))
- feature_counts: float32 [32, 128], replicated
The draws below stay inside these ranges and needn't reach their ends.
Inputs may be any that keep to these rules, and one draw needn't show every extreme that they name: `successors`: entry 0 of a block's row is the block itself; entries 1 to 4 are blocks below the device's partition size; the last 3 entries are 32 or more and name received slots. `part_sizes`: some device holds 32 blocks. `outgoing_block_list`: every entry is below the sending device's partition size. `destinations`: each is a state of a block below its device's partition size.
All inputs are finite; a program needn't handle non-finite values.
Results may differ from the reference program's by a relative error of at most 0.0014.
The reference program's roundings to bfloat16 on the way count: a program that leaves them out, or rounds other values in their place, can miss the bound.
Values may be sent and summed in bfloat16 or wider, within the bound.
No kernel may reach another device: no remote copies, remote signals or barrier semaphores. Data moves between devices by JAX's collectives and lax.ppermute only.
A program may use at most 128 MiB of HBM per device.

```python
import math
import jax
import jax.numpy as jnp
from jax import lax

BLOCK_STATES = 128
DEST_COUNT = 128
FEAT = 32
MAX_DEVICE_BLOCKS = 32
SUCC = 8
REMOTE_BLOCKS = 3
SLOTS_PER_PEER = 1
REG_DEV = 128
ITERS = 3
VISITS = 3
STATES = 131072
NBLOCKS = 1024
REGIONS = 4096
N_DOM = 8
DEVICES = 32


def chosen_full(key):
    return jax.random.randint(jax.random.fold_in(key, 12), (), 0, DEVICES)


def live_counts(key):
    counts = jax.random.randint(jax.random.fold_in(key, 11), (DEVICES,), MAX_DEVICE_BLOCKS // 2, MAX_DEVICE_BLOCKS + 1)
    return counts.at[chosen_full(key)].set(MAX_DEVICE_BLOCKS)


def draw_part_sizes(key, part):
    return live_counts(key).astype(jnp.int32)


def draw_outgoing_block_list(key, part):
    counts = live_counts(key)
    random_bits = jax.random.randint(jax.random.fold_in(key, 21), (DEVICES, N_DOM, SLOTS_PER_PEER), 0, 1 << 30)
    block_lists = random_bits % counts[:, None, None]
    return block_lists.at[chosen_full(key), 0, 0].set(MAX_DEVICE_BLOCKS - 1).astype(jnp.int32)


def draw_successors(key, part):
    counts = live_counts(key)
    nlocal = SUCC - REMOTE_BLOCKS
    slot_count = N_DOM * SLOTS_PER_PEER
    random_bits = jax.random.randint(jax.random.fold_in(key, 31), (DEVICES, MAX_DEVICE_BLOCKS, nlocal - 1), 0, 1 << 30)
    local_part = random_bits % counts[:, None, None]
    itself = jnp.broadcast_to(jnp.arange(MAX_DEVICE_BLOCKS, dtype=jnp.int32)[None, :, None], (DEVICES, MAX_DEVICE_BLOCKS, 1))
    send_orders = jax.vmap(lambda random_subkey: jax.random.permutation(random_subkey, slot_count))(jax.random.split(jax.random.fold_in(key, 32), DEVICES))
    slot_positions = (jnp.arange(MAX_DEVICE_BLOCKS)[:, None] * REMOTE_BLOCKS + jnp.arange(REMOTE_BLOCKS)[None, :]) % slot_count
    remote_part = MAX_DEVICE_BLOCKS + send_orders[:, slot_positions]
    successor_table = jnp.concatenate([itself, local_part.astype(jnp.int32), remote_part.astype(jnp.int32)], axis=2)
    return successor_table.reshape(DEVICES * MAX_DEVICE_BLOCKS, SUCC).astype(jnp.int32)


def draw_destinations(key, part):
    counts = live_counts(key)
    owners = jax.random.randint(jax.random.fold_in(key, 41), (DEST_COUNT,), 0, DEVICES)
    random_bits = jax.random.randint(jax.random.fold_in(key, 42), (DEST_COUNT,), 0, 1 << 30)
    blocks = random_bits % counts[owners]
    offsets = jax.random.randint(jax.random.fold_in(key, 43), (DEST_COUNT,), 0, BLOCK_STATES)
    return ((owners * MAX_DEVICE_BLOCKS + blocks) * BLOCK_STATES + offsets).astype(jnp.int32)


def draw_coarse(key, part):
    return 2.0 * jax.random.truncated_normal(jax.random.fold_in(key, 53), -4.0, 4.0, (REGIONS, DEST_COUNT), jnp.float32)


def with_ends(values, stream_key, low, largest):
    dims = values.shape
    index_at = [jax.random.randint(jax.random.fold_in(stream_key, axis), (), 0, dims[axis]) for axis in range(len(dims))]
    values = values.at[tuple(index_at)].set(low)
    longest = dims.index(max(dims))
    index_at[longest] = (index_at[longest] + 1) % dims[longest]
    return values.at[tuple(index_at)].set(largest)


def block_levels(stream_key, dims, cuts, smallest, top_value):
    level, own = 1.0, jax.random.fold_in(stream_key, 6)
    for axis_at, shards_of in cuts:
        heights = jnp.exp(jax.random.uniform(jax.random.fold_in(own, axis_at), (shards_of,), jnp.float32, smallest / len(cuts), top_value / len(cuts)))
        level = level * jnp.repeat(heights, dims[axis_at] // shards_of).reshape([-1 if axis == axis_at else 1 for axis in range(len(dims))])
    return level


def centred(key, shape, width, bound, kind=jnp.bfloat16):
    entries = width * jax.random.normal(key, shape, jnp.float32)
    return jnp.clip(entries, min=-bound, max=bound).astype(kind)


def setup_inputs(seed: int = 0) -> dict:
    key_list = jax.random.split(jax.random.key(seed), 11)
    return {
        "coarse": draw_coarse(jax.random.fold_in(key_list[10], 71), 0),
        "region_map": with_ends(jax.random.randint(key_list[1], (STATES,), 0, REG_DEV * N_DOM), jax.random.fold_in(key_list[1], 1), 0, (REG_DEV * N_DOM) - 1).astype(jnp.int32),
        "features": jnp.clip(1.0 * jax.random.uniform(key_list[2], (FEAT, STATES), jnp.float32) ** block_levels(key_list[2], (FEAT, STATES), ((1, 32),), -0.2, 0.2), 0.0, 1.0).astype(jnp.bfloat16),
        "reward_weights": centred(key_list[3], (FEAT,), FEAT ** -0.5, 1.0, jnp.float32),
        "transitions": jnp.clip(jnp.exp(math.log(0.0009994507) - 2.998599 * jax.random.uniform(key_list[4], (NBLOCKS, SUCC, BLOCK_STATES, BLOCK_STATES), jnp.float32) ** block_levels(key_list[4], (NBLOCKS, SUCC, BLOCK_STATES, BLOCK_STATES), ((0, 32),), -0.2, 0.2)), 4.982948303222656e-05, 0.0009994507).astype(jnp.bfloat16),
        "successors": draw_successors(jax.random.fold_in(key_list[10], 71), 0),
        "part_sizes": draw_part_sizes(jax.random.fold_in(key_list[10], 71), 0),
        "outgoing_block_list": draw_outgoing_block_list(jax.random.fold_in(key_list[10], 71), 0),
        "destinations": draw_destinations(jax.random.fold_in(key_list[10], 71), 0),
        "anchors": jnp.clip(0.099609375 + 0.9003906 * jax.random.uniform(key_list[9], (STATES, DEST_COUNT), jnp.float32) ** block_levels(key_list[9], (STATES, DEST_COUNT), ((0, 32),), -0.2, 0.2), 0.099609375, 1.0).astype(jnp.bfloat16),
    }


def block_backup(lookup, transitions, successors):
    widened = lookup.astype(jnp.float32)
    maxima = jnp.max(widened, axis=1)
    exp_weights = jnp.exp(widened - maxima[:, None, :]).astype(jnp.bfloat16)
    chosen = exp_weights[successors]
    products = jnp.einsum("bkij,bkjd->bkid", transitions.astype(jnp.float32), chosen.astype(jnp.float32))
    log_terms = maxima[successors][:, :, None, :] + jnp.log(products)
    highest = jnp.max(log_terms, axis=1)
    backed = highest + jnp.log(jnp.sum(jnp.exp(log_terms - highest[:, None]), axis=1))
    return backed, maxima, exp_weights


def forward_terms(mass_now, backed, maxima, transitions, successors):
    scaling = jnp.exp(maxima[successors][:, :, None, :] - backed[:, None, :, :])
    scaled = (mass_now[:, None] * scaling).astype(jnp.bfloat16)
    contrib = jnp.einsum("bkij,bkid->bkjd", transitions.astype(jnp.float32), scaled.astype(jnp.float32))
    empty = jnp.zeros((MAX_DEVICE_BLOCKS + N_DOM * SLOTS_PER_PEER, BLOCK_STATES, DEST_COUNT), jnp.float32)
    return empty.at[successors].add(contrib)


def add_returned(block_sums, targets, extra):
    return block_sums.at[targets.reshape(-1)].add(extra.astype(jnp.float32))


def reference(coarse, region_map, features, reward_weights, transitions, successors, part_sizes, outgoing_block_list, destinations, anchors):
    slot_count = N_DOM * SLOTS_PER_PEER
    state_ids = jnp.arange(STATES, dtype=jnp.int32)
    owner_ids = state_ids // (MAX_DEVICE_BLOCKS * BLOCK_STATES)
    region_ids = (owner_ids // N_DOM) * (REG_DEV * N_DOM) + region_map
    live_rows = (((state_ids // BLOCK_STATES) % MAX_DEVICE_BLOCKS) < part_sizes[owner_ids])[:, None]
    at_dest = state_ids[:, None] == destinations[None, :]
    rewards = jnp.dot(reward_weights[None, :], features.astype(jnp.float32), precision=lax.Precision.HIGHEST)[0]
    current_values = jnp.where(at_dest, 0.0, coarse[region_ids]).astype(jnp.bfloat16)
    block_shape = (DEVICES, MAX_DEVICE_BLOCKS, BLOCK_STATES, DEST_COUNT)
    current_values = current_values.reshape(block_shape)
    dest_blocks = at_dest.reshape(block_shape)
    reward_blocks = rewards.reshape(DEVICES, MAX_DEVICE_BLOCKS, BLOCK_STATES, 1)
    trans_blocks = transitions.reshape(DEVICES, MAX_DEVICE_BLOCKS, SUCC, BLOCK_STATES, BLOCK_STATES)
    succ_blocks = successors.reshape(DEVICES, MAX_DEVICE_BLOCKS, SUCC)
    device_ids = jnp.arange(DEVICES, dtype=jnp.int32)
    sender_devices = (device_ids // N_DOM * N_DOM)[:, None] + jnp.arange(N_DOM, dtype=jnp.int32)[None, :]
    own_dom = device_ids % N_DOM
    wanted_blocks = outgoing_block_list[sender_devices, own_dom[:, None], :]
    slot_indices = own_dom[:, None, None] * SLOTS_PER_PEER + jnp.arange(SLOTS_PER_PEER, dtype=jnp.int32)[None, None, :]
    for sweep in range(ITERS):
        received_blocks = current_values[sender_devices[:, :, None], wanted_blocks].reshape(DEVICES, slot_count, BLOCK_STATES, DEST_COUNT)
        lookup = jnp.concatenate([current_values, received_blocks], axis=1)
        backed, maxima, exp_weights = lax.map(lambda parts: block_backup(*parts), (lookup, trans_blocks, succ_blocks))
        current_values = jnp.where(dest_blocks, 0.0, reward_blocks + backed).astype(jnp.bfloat16)
    mass_now = jnp.where(live_rows, anchors.astype(jnp.float32), 0.0).reshape(block_shape)
    visits = jnp.zeros(block_shape, jnp.float32)
    for sweep in range(VISITS):
        gathered = lax.map(lambda parts: forward_terms(*parts), (mass_now, backed, maxima, trans_blocks, succ_blocks))
        outgoing_parcels = gathered[:, MAX_DEVICE_BLOCKS:].astype(jnp.bfloat16)
        returned_parcels = outgoing_parcels[sender_devices[:, :, None], slot_indices].reshape(DEVICES, slot_count, BLOCK_STATES, DEST_COUNT)
        incoming = jax.vmap(add_returned)(gathered[:, :MAX_DEVICE_BLOCKS], outgoing_block_list, returned_parcels)
        mass_now = exp_weights[:, :MAX_DEVICE_BLOCKS].astype(jnp.float32) * incoming
        visits = visits + mass_now
    values_out = jnp.where(live_rows, current_values.reshape(STATES, DEST_COUNT), 0.0).astype(jnp.bfloat16)
    visits_out = jnp.where(live_rows, visits.reshape(STATES, DEST_COUNT), 0.0).astype(jnp.bfloat16)
    totals = jnp.dot(features, visits_out, preferred_element_type=jnp.float32)
    total_mass = jnp.sum(jnp.where(live_rows, anchors.astype(jnp.float32), 0.0), axis=0)
    return values_out, visits_out, totals / total_mass[None, :]
```

```python
import jax
import jax.numpy as jnp
from jax import lax
from jax.experimental import pallas as pl
from jax.experimental.pallas import tpu as pltpu
from jax.sharding import PartitionSpec as P

ITERS = 3
VISITS = 3
REMOTE = 3
EXTRA = 16
UNIT = 8
ANY = pl.BlockSpec(memory_space=pltpu.HBM)
VMEM = pl.BlockSpec(memory_space=pltpu.VMEM)
SMEM = pl.BlockSpec(memory_space=pltpu.SMEM)
F32 = jnp.float32
BF16 = jnp.bfloat16
I32 = jnp.int32


def sds(shape, dtype):
    return jax.ShapeDtypeStruct(tuple(shape), dtype)


def mm(a, b):
    return jnp.dot(a, b, preferred_element_type=F32)


def mm_t(a, b):
    return lax.dot_general(a, b, (((0,), (0,)), ((), ())), preferred_element_type=F32)


def call(body, ins, outs, scratch, mib, flops, nbytes, name):
    return pl.pallas_call(
        body,
        out_shape=tuple(sds(shape, dtype) for _, shape, dtype in outs),
        in_specs=list(ins),
        out_specs=tuple(space for space, _, _ in outs),
        scratch_shapes=scratch,
        compiler_params=pltpu.CompilerParams(vmem_limit_bytes=mib << 20),
        cost_estimate=pl.CostEstimate(flops=flops, bytes_accessed=nbytes, transcendentals=0),
        name=name,
    )


def divisor(n, most):
    while n % most:
        most -= 1
    return most


def in_units(n, fn, before=None):
    step = divisor(n, UNIT)

    def turn(g):
        if before is not None:
            before(g)
        for i in range(step):
            fn(g * step + i)

    if n == step:
        turn(0)
        return

    @pl.loop(0, n // step)
    def _(g):
        turn(g)


def scale_rows(tops):
    peak = tops[0]
    for t in tops[1:]:
        peak = jnp.maximum(peak, t)
    return peak, [jnp.exp(t - peak) for t in tops]


def weigh(values):
    wide = values.astype(F32)
    top = jnp.max(wide, axis=0, keepdims=True)
    return jnp.exp(wide - top).astype(BF16), top


class Copies:
    def __init__(self, sem):
        self.sem, self.used = sem, 0

    def add(self, src, dst):
        at = self.used
        self.used += 1
        copy = pltpu.make_async_copy(src, dst, self.sem.at[at])
        copy.start()
        return copy


def make_kernels(nb, nsucc, s, d, slots, n_dom, rdev):
    local = nsucc - REMOTE
    nl = nb + slots
    per_peer = slots // n_dom
    blk = s * d
    pair = 2 * s * s * d
    step = divisor(nb, UNIT)
    turns = nb // step
    rows = nl + nb
    at_succ = 4
    at_listed = at_succ + nb * nsucc
    at_lead = at_listed + slots
    at_owner = at_lead + slots
    at_free = at_owner + slots

    def const_spec():
        return pltpu.VMEM((s + 8, 128), F32)

    def sems(n):
        return pltpu.SemaphoreType.DMA((n,))

    def new_values(backed, b, cst):
        sub = lax.broadcasted_iota(I32, (s, d), 0).astype(F32)
        here = sub == (cst[s : s + 1] - lax.convert_element_type(b * s, F32))
        lane = lax.broadcasted_iota(I32, (s, 128), 1)
        reward = jnp.sum(jnp.where(lane == b, cst[0:s], 0.0), axis=1, keepdims=True)
        return jnp.where(here, 0.0, reward + backed).astype(BF16)

    def chunks(sem, row, parts):
        def at(g, i):
            src, dst = parts[i](pl.ds(g * step, step))
            return pltpu.make_async_copy(src, dst, sem.at[row + i, g])

        def start(g):
            for i in range(len(parts)):
                at(g, i).start()

        def wait(g):
            for i in range(len(parts)):
                at(g, i).wait()

        return start, wait

    def start_all(start):
        for g in range(turns):
            start(g)

    def wait_all(wait):
        for g in range(turns):
            wait(g)

    def t_part(t_hbm, t_ref, k0, k1):
        return lambda at: (t_hbm.at[at, pl.ds(k0, k1 - k0)], t_ref.at[at])

    def in_part(src, dst):
        return lambda at: (src.at[at], dst.at[at])

    def pack_body(info, coarse, reg, out):
        table = coarse[...].astype(BF16)
        row = lax.broadcasted_iota(I32, (EXTRA, s), 0)
        for i in range(n_dom):
            out[i, 0:rdev] = table
            for j in range(per_peer):
                b = info[at_listed + i * per_peer + j]
                r = reg[pl.ds(b, 1)]
                high = lax.shift_right_logical(r, 7)
                low = jnp.bitwise_and(r, 127)
                extra = jnp.where(row == 0, high, jnp.where(row == 1, low, b))
                out[i, rdev + j * EXTRA : rdev + (j + 1) * EXTRA] = extra.astype(F32).astype(BF16)

    pack = call(
        pack_body, [SMEM, VMEM, VMEM],
        [(VMEM, (n_dom, rdev + per_peer * EXTRA, d), BF16)],
        [], 8, blk, 1 << 20, "pack",
    )

    def begin_body(
        info, rec, reg, cst_hbm, t_hbm, w_out, top_out, sent,
        w0, top0, table, regs, regs_t, where_d, cst, t_ref, sem, t_sem,
    ):
        cps = Copies(sem)
        got_cst = cps.add(cst_hbm, cst)
        for i in range(slots):
            pltpu.make_async_copy(t_hbm.at[info[at_listed + i]], t_ref.at[i], t_sem.at[i]).start()
        for i in range(n_dom):
            table[i * rdev : (i + 1) * rdev] = rec[i, 0:rdev]
        regs[...] = jnp.zeros_like(regs)
        regs[0:nb] = reg[...].astype(F32)
        got_cst.wait()
        own_d = cst[s : s + 1]
        for b in range(nb):
            where_d[b : b + 1] = own_d - float(b * s)
        for i in range(n_dom):
            for j in range(per_peer):
                k = nb + i * per_peer + j
                extra = rec[i, rdev + j * EXTRA : rdev + (j + 1) * EXTRA].astype(F32)
                regs[k : k + 1] = extra[0:1] * 128.0 + extra[1:2]
                shift = lax.convert_element_type(info[0] - (info[1] + i) * (nb * s), F32)
                where_d[k : k + 1] = own_d + shift - extra[2:3] * float(s)
        regs_t[...] = regs[...].T
        group = divisor(nl, 4)

        @pl.loop(0, nl // group)
        def _(g):
            lane_k = lax.broadcasted_iota(I32, (s, 128), 1)
            lane_f = lax.broadcasted_iota(I32, (s, rdev), 1).astype(F32)
            sub = lax.broadcasted_iota(I32, (s, d), 0).astype(F32)
            hot = []
            for u in range(group):
                col = jnp.sum(
                    jnp.where(lane_k == g * group + u, regs_t[...], 0.0), axis=1, keepdims=True
                )
                hot.append(
                    jnp.concatenate(
                        [
                            jnp.where(lane_f == (col - float(c * rdev)), 1.0, 0.0).astype(BF16)
                            for c in range(n_dom)
                        ],
                        axis=1,
                    )
                )
            picked = mm(jnp.concatenate(hot, axis=0), table[...])
            for u in range(group):
                k = g * group + u
                here = sub == where_d[pl.ds(k, 1)]
                w, top = weigh(jnp.where(here, 0.0, picked[u * s : (u + 1) * s]))
                w0[k] = w
                top0[pl.ds(k, 1)] = top

        put_w = cps.add(w0, w_out)
        put_top = cps.add(top0, top_out)
        for i in range(slots):
            pltpu.make_async_copy(t_hbm.at[info[at_listed + i]], t_ref.at[i], t_sem.at[i]).wait()

        def one(i):
            b = info[at_listed + i]
            peak, acc = all_terms(b, info, lambda k: t_ref[i, k], w0, top0)
            sent[i] = new_values(peak + jnp.log(acc), b, cst)

        in_units(slots, one)
        put_w.wait()
        put_top.wait()

    def all_terms(b, info, t_of, w_ref, top_ref, count=nsucc):
        es = [info[at_succ + b * nsucc + k] for k in range(count)]
        peak, sc = scale_rows([top_ref[pl.ds(e, 1)] for e in es])
        acc = mm(t_of(0), w_ref[es[0]]) * sc[0]
        for k in range(1, count):
            acc = acc + mm(t_of(k), w_ref[es[k]]) * sc[k]
        return peak, acc

    def remote_terms(b, info, t_of, w_ref, top_ref, peak0, acc0):
        es = [info[at_succ + b * nsucc + local + k] - nb for k in range(REMOTE)]
        peak, sc = scale_rows([peak0] + [top_ref[pl.ds(e, 1)] for e in es])
        acc = acc0 * sc[0]
        for k in range(REMOTE):
            acc = acc + mm(t_of(k), w_ref[es[k]]) * sc[k + 1]
        return peak, acc

    begin = call(
        begin_body, [SMEM, VMEM, VMEM, ANY, ANY],
        [(ANY, (nl, s, d), BF16), (ANY, (nl, d), F32), (VMEM, (slots, s, d), BF16)],
        [
            pltpu.VMEM((nl, s, d), BF16), pltpu.VMEM((nl, d), F32),
            pltpu.VMEM((n_dom * rdev, d), BF16), pltpu.VMEM((128, s), F32),
            pltpu.VMEM((s, 128), F32), pltpu.VMEM((nl, d), F32), const_spec(),
            pltpu.VMEM((slots, nsucc, s, s), BF16), sems(3), sems(slots),
        ],
        32, 2 * nl * s * n_dom * rdev * d + slots * nsucc * pair, 4 << 20, "begin",
    )

    def finish_local(info, t_ref, w_ref, top_ref, acc, peak, accl, acc_out, peak_out, put, sem, n0):
        def two(b):
            top, a = all_terms(b, info, lambda k: t_ref[b, k], w_ref, top_ref, local)
            acc[b] = a
            peak[pl.ds(b, 1)] = top

        def before(g):
            @pl.when(g > 0)
            def _():
                put(g - 1)

        in_units(nb, two, before)
        put(turns - 1)
        put_peak = pltpu.make_async_copy(peak, peak_out, sem.at[n0])
        put_peak.start()
        for i in range(slots):
            b = info[at_listed + i]
            accl[i, 0:s] = acc[b]
            accl[i, s : s + 8] = jnp.broadcast_to(peak[pl.ds(b, 1)], (8, d))
        put_peak.wait()

    def sweep_first_body(
        info, cst_hbm, t_hbm, w_hbm, top_hbm, acc_out, peak_out, accl,
        cst, t_ref, w0, top0, w1, top1, acc, peak, sem, c_sem,
    ):
        cps = Copies(sem)
        early = [cps.add(w_hbm, w0), cps.add(top_hbm, top0), cps.add(cst_hbm, cst)]
        start, wait = chunks(c_sem, 0, [t_part(t_hbm, t_ref, 0, nsucc)])
        put, put_wait = chunks(c_sem, 1, [lambda at: (acc.at[at], acc_out.at[at])])
        start_all(start)
        for c in early:
            c.wait()

        def one(b):
            top_all, a = all_terms(b, info, lambda k: t_ref[b, k], w0, top0)
            w, top = weigh(new_values(top_all + jnp.log(a), b, cst))
            w1[b] = w
            top1[pl.ds(b, 1)] = top

        in_units(nb, one, wait)
        finish_local(info, t_ref, w1, top1, acc, peak, accl, acc_out, peak_out, put, sem, 3)
        wait_all(put_wait)

    sweep_first = call(
        sweep_first_body, [SMEM, ANY, ANY, ANY, ANY],
        [(ANY, (nb, s, d), F32), (ANY, (nb, d), F32), (VMEM, (slots, s + 8, d), F32)],
        [
            const_spec(), pltpu.VMEM((nb, nsucc, s, s), BF16),
            pltpu.VMEM((nl, s, d), BF16), pltpu.VMEM((nl, d), F32),
            pltpu.VMEM((nb, s, d), BF16), pltpu.VMEM((nb, d), F32),
            pltpu.VMEM((nb, s, d), F32), pltpu.VMEM((nb, d), F32),
            sems(4), pltpu.SemaphoreType.DMA((2, turns)),
        ],
        40, nb * (nsucc + local) * pair, 12 << 20, "sweep_first",
    )

    def listed_next_body(info, got, accl, cst_hbm, t_hbm, sent, wr_out, cst, t_ref, topr, sem, t_sem):
        cps = Copies(sem)
        got_cst = cps.add(cst_hbm, cst)

        def cp(i):
            return pltpu.make_async_copy(
                t_hbm.at[info[at_listed + i], pl.ds(local, REMOTE)], t_ref.at[i], t_sem.at[i]
            )

        for i in range(slots):
            cp(i).start()
        for i in range(slots):
            w, top = weigh(got[i])
            wr_out[i, 0:s] = w
            wr_out[i, s : s + 16] = jnp.broadcast_to(top, (16, d)).astype(BF16)
            topr[i : i + 1] = top
        got_cst.wait()
        for i in range(slots):
            cp(i).wait()

        def one(i):
            b = info[at_listed + i]
            wr = WeightView(wr_out, s)
            peak, acc = remote_terms(
                b, info, lambda k: t_ref[i, k], wr, topr, accl[i, s : s + 1], accl[i, 0:s]
            )
            sent[i] = new_values(peak + jnp.log(acc), b, cst)

        in_units(slots, one)

    listed_next = call(
        listed_next_body, [SMEM, VMEM, VMEM, ANY, ANY],
        [(VMEM, (slots, s, d), BF16), (VMEM, (slots, s + 16, d), BF16)],
        [
            const_spec(), pltpu.VMEM((slots, REMOTE, s, s), BF16), pltpu.VMEM((slots, d), F32),
            sems(1), sems(slots),
        ],
        16, slots * REMOTE * pair, 3 << 20, "listed_next",
    )

    def sweep_next_body(
        info, wr, cst_hbm, t_hbm, acc_hbm, peak_hbm, w_out, top_out, acc_out, peak_out, wl_out,
        cst, t_ref, acc_in, peak_in, w2, top2, topr, acc, peak, accl, sem, c_sem,
    ):
        cps = Copies(sem)
        early = [cps.add(cst_hbm, cst), cps.add(peak_hbm, peak_in)]
        start, wait = chunks(
            c_sem, 0, [t_part(t_hbm, t_ref, 0, nsucc), in_part(acc_hbm, acc_in)]
        )
        put_w, put_w_wait = chunks(c_sem, 2, [lambda at: (w2.at[at], w_out.at[at])])
        put, put_wait = chunks(c_sem, 3, [lambda at: (acc.at[at], acc_out.at[at])])
        start_all(start)
        for i in range(slots):
            topr[i : i + 1] = wr[i, s : s + 1].astype(F32)
        for c in early:
            c.wait()

        def one(b):
            top_all, a = remote_terms(
                b, info, lambda k: t_ref[b, local + k], WeightView(wr, s), topr,
                peak_in[pl.ds(b, 1)], acc_in[b],
            )
            w, top = weigh(new_values(top_all + jnp.log(a), b, cst))
            w2[b] = w
            top2[pl.ds(b, 1)] = top

        in_units(nb, one, wait)
        start_all(put_w)
        put_top = cps.add(top2, top_out)
        finish_local(info, t_ref, w2, top2, acc, peak, accl, acc_out, peak_out, put, sem, 3)
        for i in range(slots):
            wl_out[i] = w2[info[at_listed + i]]
        put_top.wait()
        wait_all(put_w_wait)
        wait_all(put_wait)

    sweep_next = call(
        sweep_next_body, [SMEM, VMEM, ANY, ANY, ANY, ANY],
        [
            (ANY, (nb, s, d), BF16), (ANY, (nb, d), F32), (ANY, (nb, s, d), F32),
            (ANY, (nb, d), F32), (VMEM, (slots, s, d), BF16),
        ],
        [
            const_spec(), pltpu.VMEM((nb, nsucc, s, s), BF16),
            pltpu.VMEM((nb, s, d), F32), pltpu.VMEM((nb, d), F32),
            pltpu.VMEM((nb, s, d), BF16), pltpu.VMEM((nb, d), F32), pltpu.VMEM((slots, d), F32),
            pltpu.VMEM((nb, s, d), F32), pltpu.VMEM((nb, d), F32),
            pltpu.VMEM((slots, s + 8, d), F32),
            sems(4), pltpu.SemaphoreType.DMA((4, turns)),
        ],
        40, nb * nsucc * pair, 14 << 20, "sweep_next",
    )

    def add_flows(b, r, info, t_of, k0, k1, row, acc, base):
        peak = row[pl.ds(nl + b, 1)]
        for k in range(k0, k1):
            e = info[at_succ + b * nsucc + k]
            sc = jnp.exp(row[pl.ds(e, 1)] - peak)
            acc[e - base] = acc[e - base] + mm_t(t_of(k - k0), r) * sc

    def last_body(
        info, got, cst_hbm, t_hbm, acc_hbm, peak_hbm, top_hbm, anc_hbm,
        val_out, inv_out, r_out, row_out, sent, invl,
        cst, t_ref, acc_in, peak_in, row, anc, val, inv, r, wr, topr, slot_acc, sem, c_sem,
    ):
        cps = Copies(sem)
        early = [
            cps.add(cst_hbm, cst), cps.add(peak_hbm, peak_in), cps.add(top_hbm, row.at[pl.ds(0, nb)])
        ]
        start, wait = chunks(
            c_sem, 0,
            [t_part(t_hbm, t_ref, local, nsucc), in_part(acc_hbm, acc_in), in_part(anc_hbm, anc)],
        )
        put, put_wait = chunks(
            c_sem, 3,
            [in_part(val, val_out), in_part(inv, inv_out), in_part(r, r_out)],
        )
        start_all(start)
        slot_acc[...] = jnp.zeros_like(slot_acc)
        for i in range(slots):
            w, top = weigh(got[i])
            wr[i] = w
            topr[i : i + 1] = top
        for c in early:
            c.wait()
        row[nb:nl] = topr[...]

        def one(b):
            top_all, a = remote_terms(
                b, info, lambda k: t_ref[b, k], wr, topr, peak_in[pl.ds(b, 1)], acc_in[b]
            )
            row[pl.ds(nl + b, 1)] = top_all
            live = b < info[2]
            v = new_values(top_all + jnp.log(a), b, cst)
            val[b] = jnp.where(live, v.astype(F32), 0.0).astype(BF16)
            share = jnp.where(live, 1.0 / a, 0.0)
            inv[b] = share
            r[b] = (anc[b].astype(F32) * share).astype(BF16)

        in_units(nb, one, wait)
        start_all(put)
        put_row = cps.add(row, row_out)

        def two(b):
            add_flows(b, r[b], info, lambda k: t_ref[b, k], local, nsucc, row, slot_acc, nb)

        in_units(nb, two)
        sent[...] = slot_acc[...].astype(BF16)
        for i in range(slots):
            invl[i] = inv[info[at_listed + i]]
        put_row.wait()
        wait_all(put_wait)

    last = call(
        last_body, [SMEM, VMEM, ANY, ANY, ANY, ANY, ANY, ANY],
        [
            (ANY, (nb, s, d), BF16), (ANY, (nb, s, d), F32), (ANY, (nb, s, d), BF16),
            (ANY, (rows, d), F32), (VMEM, (slots, s, d), BF16), (VMEM, (slots, s, d), F32),
        ],
        [
            const_spec(), pltpu.VMEM((nb, REMOTE, s, s), BF16),
            pltpu.VMEM((nb, s, d), F32), pltpu.VMEM((nb, d), F32), pltpu.VMEM((rows, d), F32),
            pltpu.VMEM((nb, s, d), BF16), pltpu.VMEM((nb, s, d), BF16),
            pltpu.VMEM((nb, s, d), F32), pltpu.VMEM((nb, s, d), BF16),
            pltpu.VMEM((slots, s, d), BF16), pltpu.VMEM((slots, d), F32),
            pltpu.VMEM((slots, s, d), F32),
            sems(4), pltpu.SemaphoreType.DMA((6, turns)),
        ],
        40, nb * 2 * REMOTE * pair, 14 << 20, "last",
    )

    def make_spread(first, final):
        ks = local if final else nsucc

        def body(*refs):
            refs = list(refs)
            info = refs.pop(0)
            r_listed = None if first else refs.pop(0)
            row_hbm, t_hbm, r_hbm, w_hbm = refs[:4]
            refs = refs[4:]
            inv_hbm = None if final else refs.pop(0)
            total_hbm = None if first else refs.pop(0)
            if final:
                vis_out, totl = refs[:2]
                refs = refs[2:]
            else:
                total_out, r_out, ownl, part = refs[:4]
                refs = refs[4:]
            row, t_ref, r_in, w2, total, own, sem, c_sem = refs[:8]
            refs = refs[8:]
            if final:
                vis = refs.pop(0)
            else:
                inv, r_next = refs
            get_row = pltpu.make_async_copy(row_hbm, row, sem.at[0])
            get_row.start()
            start, wait = chunks(c_sem, 0, [t_part(t_hbm, t_ref, 0, ks)])
            r_start, r_wait = chunks(c_sem, 1, [in_part(r_hbm, r_in)])
            later = [in_part(w_hbm, w2)]
            if not final:
                later.append(in_part(inv_hbm, inv))
            if not first:
                later.append(in_part(total_hbm, total))
            late_start, late_wait = chunks(c_sem, 2, later)
            if final:
                out_parts = [in_part(vis, vis_out)]
            else:
                out_parts = [in_part(own if first else total, total_out), in_part(r_next, r_out)]
            put, put_wait = chunks(c_sem, 5, out_parts)
            start_all(r_start)
            start_all(start)
            start_all(late_start)
            own[...] = jnp.zeros_like(own)
            wait_all(r_wait)
            if not first:
                for i in range(slots):
                    @pl.when(info[at_lead + i] == 1)
                    def _(i=i):
                        r_in[info[at_listed + i]] = r_listed[i]
            get_row.wait()

            def one(b):
                add_flows(b, r_in[b], info, lambda k: t_ref[b, k], 0, local, row, own, 0)

            in_units(nb, one, wait)
            if not final:
                part[...] = jnp.zeros_like(part)

            def before(g):
                late_wait(g)

                @pl.when(g > 0)
                def _():
                    put(g - 1)

            def two(b):
                if final:
                    sums = total[b] + own[b]
                    own[b] = sums
                    mass = jnp.where(b < info[2], w2[b].astype(F32) * sums, 0.0)
                    vis[b] = mass.astype(BF16)
                    return
                free = lax.convert_element_type(info[at_free + b], F32)
                r = (w2[b].astype(F32) * own[b] * (inv[b] * free)).astype(BF16)
                r_next[b] = r
                if not first:
                    total[b] = total[b] + own[b]
                add_flows(b, r, info, lambda k: t_ref[b, local + k], local, nsucc, row, part, nb)

            in_units(nb, two, before)
            put(turns - 1)
            for i in range(slots):
                if final:
                    totl[i] = own[info[at_listed + i]]
                else:
                    ownl[i] = own[info[at_listed + i]]
            wait_all(put_wait)

        if final:
            outs = [(ANY, (nb, s, d), BF16), (VMEM, (slots, s, d), F32)]
        else:
            outs = [
                (ANY, (nb, s, d), F32), (ANY, (nb, s, d), BF16),
                (VMEM, (slots, s, d), F32), (VMEM, (slots, s, d), F32),
            ]
        ins = [SMEM] + ([] if first else [VMEM]) + [ANY] * 4
        ins += ([] if final else [ANY]) + ([] if first else [ANY])
        scratch = [
            pltpu.VMEM((rows, d), F32), pltpu.VMEM((nb, ks, s, s), BF16),
            pltpu.VMEM((nb, s, d), BF16), pltpu.VMEM((nb, s, d), BF16),
            pltpu.VMEM((nb, s, d), F32), pltpu.VMEM((nb, s, d), F32),
            sems(1), pltpu.SemaphoreType.DMA((7, turns)),
        ]
        if final:
            scratch.append(pltpu.VMEM((nb, s, d), BF16))
        else:
            scratch += [pltpu.VMEM((nb, s, d), F32), pltpu.VMEM((nb, s, d), BF16)]
        return call(body, ins, outs, scratch, 40, nb * ks * pair, 14 << 20, "spread")

    def make_join(first):
        def body(*refs):
            refs = list(refs)
            info, got, ownl, invl, wl, part, row_hbm, t_hbm = refs[:8]
            refs = refs[8:]
            back_in = None if first else refs.pop(0)
            sent, r_out, back, row, t_ref, sem, t_sem = refs

            def cp(i):
                return pltpu.make_async_copy(
                    t_hbm.at[info[at_listed + i], pl.ds(local, REMOTE)], t_ref.at[i], t_sem.at[i]
                )

            get_row = pltpu.make_async_copy(row_hbm, row, sem.at[0])
            get_row.start()
            for i in range(slots):
                cp(i).start()
            add_returned(info, got, back)
            get_row.wait()
            for i in range(slots):
                cp(i).wait()
            acc = part

            def one(i):
                b = info[at_listed + i]
                here = back[i]
                leads = lax.convert_element_type(info[at_lead + i], F32)
                mass = wl[i].astype(F32) * (ownl[i] + here)
                r_out[i] = (mass * (invl[i] * leads)).astype(BF16)
                if not first:
                    back[i] = back_in[i] + here

            in_units(slots, one)
            total = [None] * slots
            del total

            def two(i):
                b = info[at_listed + i]
                add_flows(b, r_out[i], info, lambda k: t_ref[i, k], local, nsucc, row, acc, nb)

            in_units(slots, two)
            sent[...] = acc[...].astype(BF16)

        def wrapped(*refs):
            refs = list(refs)
            scratch = refs.pop()
            scratch[...] = refs[5][...]
            refs[5] = scratch
            body(*refs)

        ins = [SMEM, VMEM, VMEM, VMEM, VMEM, VMEM, ANY, ANY] + ([] if first else [VMEM])
        return call(
            wrapped, ins,
            [
                (VMEM, (slots, s, d), BF16), (VMEM, (slots, s, d), BF16), (VMEM, (slots, s, d), F32),
            ],
            [
                pltpu.VMEM((rows, d), F32), pltpu.VMEM((slots, REMOTE, s, s), BF16),
                sems(1), sems(slots), pltpu.VMEM((slots, s, d), F32),
            ],
            16, slots * REMOTE * pair, 4 << 20, "join",
        )

    def add_returned(info, got, back):
        back[...] = jnp.zeros_like(back)
        for i in range(slots):
            j = info[at_owner + i]
            back[j] = back[j] + got[i].astype(F32)

    def close_body(info, got, totl, wl, back_in, vis_in, vis_out, back, stage, sem):
        del vis_in
        back[...] = back_in[...]
        for i in range(slots):
            j = info[at_owner + i]
            back[j] = back[j] + got[i].astype(F32)
        for i in range(slots):
            stage[i] = (wl[i].astype(F32) * (totl[i] + back[i])).astype(BF16)

        def cp(i):
            return pltpu.make_async_copy(stage.at[i], vis_out.at[info[at_listed + i]], sem.at[i])

        for i in range(slots):
            @pl.when(info[at_lead + i] == 1)
            def _(i=i):
                cp(i).start()

        for i in range(slots):
            @pl.when(info[at_lead + i] == 1)
            def _(i=i):
                cp(i).wait()

    close = pl.pallas_call(
        close_body,
        out_shape=sds((nb, s, d), BF16),
        in_specs=[SMEM] + [VMEM] * 4 + [ANY],
        out_specs=ANY,
        scratch_shapes=[
            pltpu.VMEM((slots, s, d), F32), pltpu.VMEM((slots, s, d), BF16), sems(slots),
        ],
        input_output_aliases={5: 0},
        compiler_params=pltpu.CompilerParams(vmem_limit_bytes=16 << 20),
        cost_estimate=pl.CostEstimate(flops=blk, bytes_accessed=2 << 20, transcendentals=0),
        name="close",
    )

    return dict(
        pack=pack, begin=begin, sweep_first=sweep_first, listed_next=listed_next,
        sweep_next=sweep_next, last=last, spread=make_spread, join=make_join, close=close,
    )


class WeightView:
    def __init__(self, ref, rows):
        self.ref, self.rows = ref, rows

    def __getitem__(self, e):
        return self.ref[e, 0 : self.rows]


def swap(parcels, axis):
    return lax.all_to_all(parcels, axis, split_axis=0, concat_axis=0, tiled=True)


def total_over(x, axis):
    n = lax.axis_size(axis)
    return jnp.sum(swap(jnp.broadcast_to(x[None], (n,) + x.shape), axis), axis=0)


def on_device(
    coarse, region_map, features, reward_weights, transitions, successors,
    part_sizes, outgoing_block_list, destinations, anchors,
):
    nb, nsucc, s, _ = transitions.shape
    rdev, d = coarse.shape
    n_dom = lax.axis_size("dom")
    per_peer = outgoing_block_list.shape[2]
    slots = n_dom * per_peer
    feat = features.shape[0]
    grp_first = lax.axis_index("grp") * n_dom
    linear = grp_first + lax.axis_index("dom")
    ks = make_kernels(nb, nsucc, s, d, slots, n_dom, rdev)

    listed = outgoing_block_list.reshape(slots)
    same = listed[:, None] == listed[None, :]
    owner = jnp.argmax(same, axis=1).astype(I32)
    lead = (owner == jnp.arange(slots, dtype=I32)).astype(I32)
    free = 1 - jnp.any(listed[None, :] == jnp.arange(nb, dtype=I32)[:, None], axis=1).astype(I32)
    base = linear * (nb * s)
    info = jnp.concatenate(
        [
            jnp.stack([base, grp_first, part_sizes[0], jnp.int32(0)]).astype(I32),
            successors.reshape(nb * nsucc), listed, lead, owner, free,
        ]
    )
    regions = region_map.reshape(nb, s)
    (parcels,) = ks["pack"](info, coarse, regions)
    rec = swap(parcels, "dom")

    rewards = jnp.dot(
        reward_weights[None, :], features.astype(F32), precision=lax.Precision.HIGHEST
    )[0]
    cst = jnp.concatenate(
        [
            jnp.pad(rewards.reshape(nb, s).T, ((0, 0), (0, 128 - nb))),
            jnp.broadcast_to((destinations - base).astype(F32)[None, :], (8, d)),
        ],
        axis=0,
    )

    w0, top0, sent = ks["begin"](info, rec, regions, cst, transitions)
    got = swap(sent, "dom")
    acc, peak, accl = ks["sweep_first"](info, cst, transitions, w0, top0)
    sent, wr = ks["listed_next"](info, got, accl, cst, transitions)
    got = swap(sent, "dom")
    w2, top2, acc, peak, wl = ks["sweep_next"](info, wr, cst, transitions, acc, peak)
    values, inv, r, row, sent, invl = ks["last"](
        info, got, cst, transitions, acc, peak, top2, anchors.reshape(nb, s, d)
    )
    got = swap(sent, "dom")
    total, r, ownl, part = ks["spread"](True, False)(info, row, transitions, r, w2, inv)
    sent, rl, back = ks["join"](True)(info, got, ownl, invl, wl, part, row, transitions)
    got = swap(sent, "dom")
    total, r, ownl, part = ks["spread"](False, False)(
        info, rl, row, transitions, r, w2, inv, total
    )
    sent, rl, back = ks["join"](False)(info, got, ownl, invl, wl, part, row, transitions, back)
    got = swap(sent, "dom")
    visits, totl = ks["spread"](False, True)(info, rl, row, transitions, r, w2, total)
    visits = ks["close"](info, got, totl, wl, back, visits)

    values = values.reshape(nb * s, d)
    visits = visits.reshape(nb * s, d)
    live_rows = (jnp.arange(nb * s, dtype=I32) // s < part_sizes[0])[:, None]
    mass = jnp.sum(jnp.where(live_rows, anchors.astype(F32), 0.0), axis=0, keepdims=True)
    part_counts = jnp.dot(features, visits, preferred_element_type=F32)
    sums = jnp.concatenate([part_counts, jnp.broadcast_to(mass, (8, d))], axis=0)
    sums = total_over(total_over(sums, "dom"), "grp")
    return values, visits, sums[:feat] / sums[feat : feat + 1]


def solution(mesh):
    every = ("grp", "dom")
    return jax.shard_map(
        on_device,
        mesh=mesh,
        in_specs=(
            P(every, None), P(every), P(None, every), P(), P(every, None, None, None),
            P(every, None), P(every), P(every, None, None), P(), P(every, None),
        ),
        out_specs=(P(every, None), P(every, None), P()),
        check_vma=False,
    )
```

```python
import jax
import jax.numpy as jnp
from jax import lax
from jax.experimental import pallas as pl
from jax.experimental.pallas import tpu as pltpu
from jax.sharding import PartitionSpec as P

ITERS = 3
VISITS = 3
REMOTE = 3
EXTRA = 16
UNIT = 8
GRANT = 60 * 1024 * 1024
ANY = pl.BlockSpec(memory_space=pltpu.HBM)
VMEM = pl.BlockSpec(memory_space=pltpu.VMEM)
SMEM = pl.BlockSpec(memory_space=pltpu.SMEM)
F32 = jnp.float32
BF16 = jnp.bfloat16
I32 = jnp.int32


def sds(shape, dtype):
    return jax.ShapeDtypeStruct(tuple(shape), dtype)


def mm(a, b):
    return jnp.dot(a, b, preferred_element_type=F32)


def mm_t(a, b):
    return lax.dot_general(a, b, (((0,), (0,)), ((), ())), preferred_element_type=F32)


def call(body, ins, outs, scratch, flops, nbytes, name):
    return pl.pallas_call(
        body,
        out_shape=tuple(sds(shape, dtype) for _, shape, dtype in outs),
        in_specs=list(ins),
        out_specs=tuple(space for space, _, _ in outs),
        scratch_shapes=scratch,
        compiler_params=pltpu.CompilerParams(vmem_limit_bytes=GRANT),
        cost_estimate=pl.CostEstimate(flops=flops, bytes_accessed=nbytes, transcendentals=0),
        name=name,
    )


def divisor(n, most):
    while n % most:
        most -= 1
    return most


def in_units(n, fn, before=None):
    step = divisor(n, UNIT)

    def turn(g):
        if before is not None:
            before(g)
        for i in range(step):
            fn(g * step + i)

    if n == step:
        turn(0)
        return

    @pl.loop(0, n // step)
    def _(g):
        turn(g)


def scale_rows(tops):
    peak = tops[0]
    for t in tops[1:]:
        peak = jnp.maximum(peak, t)
    return peak, [jnp.exp(t - peak) for t in tops]


def weigh(values):
    wide = values.astype(F32)
    top = jnp.max(wide, axis=0, keepdims=True)
    return jnp.exp(wide - top).astype(BF16), top


class Copies:
    def __init__(self, sem):
        self.sem, self.used = sem, 0

    def add(self, src, dst):
        at = self.used
        self.used += 1
        copy = pltpu.make_async_copy(src, dst, self.sem.at[at])
        copy.start()
        return copy


def make_kernels(nb, nsucc, s, d, slots, n_dom, rdev):
    local = nsucc - REMOTE
    nl = nb + slots
    per_peer = slots // n_dom
    blk = s * d
    pair = 2 * s * s * d
    step = divisor(nb, UNIT)
    turns = nb // step
    rows = nl + nb
    at_succ = 4
    at_listed = at_succ + nb * nsucc
    at_lead = at_listed + slots
    at_owner = at_lead + slots
    at_free = at_owner + slots

    def const_spec():
        return pltpu.VMEM((s + 8, 128), F32)

    def sems(n):
        return pltpu.SemaphoreType.DMA((n,))

    def new_values(backed, b, cst):
        sub = lax.broadcasted_iota(I32, (s, d), 0).astype(F32)
        here = sub == (cst[s : s + 1] - lax.convert_element_type(b * s, F32))
        lane = lax.broadcasted_iota(I32, (s, 128), 1)
        reward = jnp.sum(jnp.where(lane == b, cst[0:s], 0.0), axis=1, keepdims=True)
        return jnp.where(here, 0.0, reward + backed).astype(BF16)

    def chunks(sem, row, parts):
        def at(g, i):
            src, dst = parts[i](pl.ds(g * step, step))
            return pltpu.make_async_copy(src, dst, sem.at[row + i, g])

        def start(g):
            for i in range(len(parts)):
                at(g, i).start()

        def wait(g):
            for i in range(len(parts)):
                at(g, i).wait()

        return start, wait

    def start_all(start):
        for g in range(turns):
            start(g)

    def wait_all(wait):
        for g in range(turns):
            wait(g)

    def t_part(t_hbm, t_ref, k0, k1):
        return lambda at: (t_hbm.at[at, pl.ds(k0, k1 - k0)], t_ref.at[at])

    def in_part(src, dst):
        return lambda at: (src.at[at], dst.at[at])

    def pack_body(info, coarse, reg, out):
        table = coarse[...].astype(BF16)
        row = lax.broadcasted_iota(I32, (EXTRA, s), 0)
        for i in range(n_dom):
            out[i, 0:rdev] = table
            for j in range(per_peer):
                b = info[at_listed + i * per_peer + j]
                r = reg[pl.ds(b, 1)]
                high = lax.shift_right_logical(r, 7)
                low = jnp.bitwise_and(r, 127)
                extra = jnp.where(row == 0, high, jnp.where(row == 1, low, b))
                out[i, rdev + j * EXTRA : rdev + (j + 1) * EXTRA] = extra.astype(F32).astype(BF16)

    pack = call(
        pack_body, [SMEM, VMEM, VMEM],
        [(VMEM, (n_dom, rdev + per_peer * EXTRA, d), BF16)],
        [], blk, 1 << 20, "pack",
    )

    def begin_body(
        info, rec, reg, cst_hbm, t_hbm, w_out, top_out, sent,
        w0, top0, table, regs, regs_t, where_d, cst, t_ref, sem, t_sem,
    ):
        cps = Copies(sem)
        got_cst = cps.add(cst_hbm, cst)
        for i in range(slots):
            pltpu.make_async_copy(t_hbm.at[info[at_listed + i]], t_ref.at[i], t_sem.at[i]).start()
        for i in range(n_dom):
            table[i * rdev : (i + 1) * rdev] = rec[i, 0:rdev]
        regs[...] = jnp.zeros_like(regs)
        regs[0:nb] = reg[...].astype(F32)
        got_cst.wait()
        own_d = cst[s : s + 1]
        for b in range(nb):
            where_d[b : b + 1] = own_d - float(b * s)
        for i in range(n_dom):
            for j in range(per_peer):
                k = nb + i * per_peer + j
                extra = rec[i, rdev + j * EXTRA : rdev + (j + 1) * EXTRA].astype(F32)
                regs[k : k + 1] = extra[0:1] * 128.0 + extra[1:2]
                shift = lax.convert_element_type(info[0] - (info[1] + i) * (nb * s), F32)
                where_d[k : k + 1] = own_d + shift - extra[2:3] * float(s)
        regs_t[...] = regs[...].T
        group = divisor(nl, 4)

        @pl.loop(0, nl // group)
        def _(g):
            lane_k = lax.broadcasted_iota(I32, (s, 128), 1)
            lane_f = lax.broadcasted_iota(I32, (s, rdev), 1).astype(F32)
            sub = lax.broadcasted_iota(I32, (s, d), 0).astype(F32)
            hot = []
            for u in range(group):
                col = jnp.sum(
                    jnp.where(lane_k == g * group + u, regs_t[...], 0.0), axis=1, keepdims=True
                )
                hot.append(
                    jnp.concatenate(
                        [
                            jnp.where(lane_f == (col - float(c * rdev)), 1.0, 0.0).astype(BF16)
                            for c in range(n_dom)
                        ],
                        axis=1,
                    )
                )
            picked = mm(jnp.concatenate(hot, axis=0), table[...])
            for u in range(group):
                k = g * group + u
                here = sub == where_d[pl.ds(k, 1)]
                w, top = weigh(jnp.where(here, 0.0, picked[u * s : (u + 1) * s]))
                w0[k] = w
                top0[pl.ds(k, 1)] = top

        put_w = cps.add(w0, w_out)
        put_top = cps.add(top0, top_out)
        for i in range(slots):
            pltpu.make_async_copy(t_hbm.at[info[at_listed + i]], t_ref.at[i], t_sem.at[i]).wait()

        def one(i):
            b = info[at_listed + i]
            peak, acc = all_terms(b, info, lambda k: t_ref[i, k], w0, top0)
            sent[i] = new_values(peak + jnp.log(acc), b, cst)

        in_units(slots, one)
        put_w.wait()
        put_top.wait()

    def all_terms(b, info, t_of, w_ref, top_ref, count=nsucc):
        es = [info[at_succ + b * nsucc + k] for k in range(count)]
        peak, sc = scale_rows([top_ref[pl.ds(e, 1)] for e in es])
        acc = mm(t_of(0), w_ref[es[0]]) * sc[0]
        for k in range(1, count):
            acc = acc + mm(t_of(k), w_ref[es[k]]) * sc[k]
        return peak, acc

    def remote_terms(b, info, t_of, w_ref, top_ref, peak0, acc0):
        es = [info[at_succ + b * nsucc + local + k] - nb for k in range(REMOTE)]
        peak, sc = scale_rows([peak0] + [top_ref[pl.ds(e, 1)] for e in es])
        acc = acc0 * sc[0]
        for k in range(REMOTE):
            acc = acc + mm(t_of(k), w_ref[es[k]]) * sc[k + 1]
        return peak, acc

    begin = call(
        begin_body, [SMEM, VMEM, VMEM, ANY, ANY],
        [(ANY, (nl, s, d), BF16), (ANY, (nl, d), F32), (VMEM, (slots, s, d), BF16)],
        [
            pltpu.VMEM((nl, s, d), BF16), pltpu.VMEM((nl, d), F32),
            pltpu.VMEM((n_dom * rdev, d), BF16), pltpu.VMEM((128, s), F32),
            pltpu.VMEM((s, 128), F32), pltpu.VMEM((nl, d), F32), const_spec(),
            pltpu.VMEM((slots, nsucc, s, s), BF16), sems(3), sems(slots),
        ],
        2 * nl * s * n_dom * rdev * d + slots * nsucc * pair, 4 << 20, "begin",
    )

    def finish_local(info, t_ref, w_ref, top_ref, acc, peak, accl, acc_out, peak_out, put, sem, n0):
        def two(b):
            top, a = all_terms(b, info, lambda k: t_ref[b, k], w_ref, top_ref, local)
            acc[b] = a
            peak[pl.ds(b, 1)] = top

        def before(g):
            @pl.when(g > 0)
            def _():
                put(g - 1)

        in_units(nb, two, before)
        put(turns - 1)
        put_peak = pltpu.make_async_copy(peak, peak_out, sem.at[n0])
        put_peak.start()
        for i in range(slots):
            b = info[at_listed + i]
            accl[i, 0:s] = acc[b]
            accl[i, s : s + 8] = jnp.broadcast_to(peak[pl.ds(b, 1)], (8, d))
        put_peak.wait()

    def sweep_first_body(
        info, cst_hbm, t_hbm, w_hbm, top_hbm, acc_out, peak_out, accl,
        cst, t_ref, w0, top0, w1, top1, acc, peak, sem, c_sem,
    ):
        cps = Copies(sem)
        early = [cps.add(w_hbm, w0), cps.add(top_hbm, top0), cps.add(cst_hbm, cst)]
        start, wait = chunks(c_sem, 0, [t_part(t_hbm, t_ref, 0, nsucc)])
        put, put_wait = chunks(c_sem, 1, [lambda at: (acc.at[at], acc_out.at[at])])
        start_all(start)
        for c in early:
            c.wait()

        def one(b):
            top_all, a = all_terms(b, info, lambda k: t_ref[b, k], w0, top0)
            w, top = weigh(new_values(top_all + jnp.log(a), b, cst))
            w1[b] = w
            top1[pl.ds(b, 1)] = top

        in_units(nb, one, wait)
        finish_local(info, t_ref, w1, top1, acc, peak, accl, acc_out, peak_out, put, sem, 3)
        wait_all(put_wait)

    sweep_first = call(
        sweep_first_body, [SMEM, ANY, ANY, ANY, ANY],
        [(ANY, (nb, s, d), F32), (ANY, (nb, d), F32), (VMEM, (slots, s + 8, d), F32)],
        [
            const_spec(), pltpu.VMEM((nb, nsucc, s, s), BF16),
            pltpu.VMEM((nl, s, d), BF16), pltpu.VMEM((nl, d), F32),
            pltpu.VMEM((nb, s, d), BF16), pltpu.VMEM((nb, d), F32),
            pltpu.VMEM((nb, s, d), F32), pltpu.VMEM((nb, d), F32),
            sems(4), pltpu.SemaphoreType.DMA((2, turns)),
        ],
        nb * (nsucc + local) * pair, 12 << 20, "sweep_first",
    )

    def listed_next_body(info, got, accl, cst_hbm, t_hbm, sent, wr_out, cst, t_ref, topr, sem, t_sem):
        cps = Copies(sem)
        got_cst = cps.add(cst_hbm, cst)

        def cp(i):
            return pltpu.make_async_copy(
                t_hbm.at[info[at_listed + i], pl.ds(local, REMOTE)], t_ref.at[i], t_sem.at[i]
            )

        for i in range(slots):
            cp(i).start()
        for i in range(slots):
            w, top = weigh(got[i])
            wr_out[i, 0:s] = w
            wr_out[i, s : s + 16] = jnp.broadcast_to(top, (16, d)).astype(BF16)
            topr[i : i + 1] = top
        got_cst.wait()
        for i in range(slots):
            cp(i).wait()

        def one(i):
            b = info[at_listed + i]
            wr = WeightView(wr_out, s)
            peak, acc = remote_terms(
                b, info, lambda k: t_ref[i, k], wr, topr, accl[i, s : s + 1], accl[i, 0:s]
            )
            sent[i] = new_values(peak + jnp.log(acc), b, cst)

        in_units(slots, one)

    listed_next = call(
        listed_next_body, [SMEM, VMEM, VMEM, ANY, ANY],
        [(VMEM, (slots, s, d), BF16), (VMEM, (slots, s + 16, d), BF16)],
        [
            const_spec(), pltpu.VMEM((slots, REMOTE, s, s), BF16), pltpu.VMEM((slots, d), F32),
            sems(1), sems(slots),
        ],
        slots * REMOTE * pair, 3 << 20, "listed_next",
    )

    def sweep_next_body(
        info, wr, cst_hbm, t_hbm, acc_hbm, peak_hbm, w_out, top_out, acc_out, peak_out, wl_out,
        cst, t_ref, acc_in, peak_in, w2, top2, topr, acc, peak, accl, sem, c_sem,
    ):
        cps = Copies(sem)
        early = [cps.add(cst_hbm, cst), cps.add(peak_hbm, peak_in)]
        start, wait = chunks(
            c_sem, 0, [t_part(t_hbm, t_ref, 0, nsucc), in_part(acc_hbm, acc_in)]
        )
        put_w, put_w_wait = chunks(c_sem, 2, [lambda at: (w2.at[at], w_out.at[at])])
        put, put_wait = chunks(c_sem, 3, [lambda at: (acc.at[at], acc_out.at[at])])
        start_all(start)
        for i in range(slots):
            topr[i : i + 1] = wr[i, s : s + 1].astype(F32)
        for c in early:
            c.wait()

        def one(b):
            top_all, a = remote_terms(
                b, info, lambda k: t_ref[b, local + k], WeightView(wr, s), topr,
                peak_in[pl.ds(b, 1)], acc_in[b],
            )
            w, top = weigh(new_values(top_all + jnp.log(a), b, cst))
            w2[b] = w
            top2[pl.ds(b, 1)] = top

        in_units(nb, one, wait)
        start_all(put_w)
        put_top = cps.add(top2, top_out)
        finish_local(info, t_ref, w2, top2, acc, peak, accl, acc_out, peak_out, put, sem, 3)
        for i in range(slots):
            wl_out[i] = w2[info[at_listed + i]]
        put_top.wait()
        wait_all(put_w_wait)
        wait_all(put_wait)

    sweep_next = call(
        sweep_next_body, [SMEM, VMEM, ANY, ANY, ANY, ANY],
        [
            (ANY, (nb, s, d), BF16), (ANY, (nb, d), F32), (ANY, (nb, s, d), F32),
            (ANY, (nb, d), F32), (VMEM, (slots, s, d), BF16),
        ],
        [
            const_spec(), pltpu.VMEM((nb, nsucc, s, s), BF16),
            pltpu.VMEM((nb, s, d), F32), pltpu.VMEM((nb, d), F32),
            pltpu.VMEM((nb, s, d), BF16), pltpu.VMEM((nb, d), F32), pltpu.VMEM((slots, d), F32),
            pltpu.VMEM((nb, s, d), F32), pltpu.VMEM((nb, d), F32),
            pltpu.VMEM((slots, s + 8, d), F32),
            sems(4), pltpu.SemaphoreType.DMA((4, turns)),
        ],
        nb * nsucc * pair, 14 << 20, "sweep_next",
    )

    def add_flows(b, r, info, t_of, k0, k1, row, acc, base):
        peak = row[pl.ds(nl + b, 1)]
        for k in range(k0, k1):
            e = info[at_succ + b * nsucc + k]
            sc = jnp.exp(row[pl.ds(e, 1)] - peak)
            acc[e - base] = acc[e - base] + mm_t(t_of(k - k0), r) * sc

    def last_body(
        info, got, cst_hbm, t_hbm, acc_hbm, peak_hbm, top_hbm, anc_hbm,
        val_out, inv_out, r_out, row_out, sent, invl,
        cst, t_ref, acc_in, peak_in, row, anc, val, inv, r, wr, topr, slot_acc, sem, c_sem,
    ):
        cps = Copies(sem)
        early = [
            cps.add(cst_hbm, cst), cps.add(peak_hbm, peak_in), cps.add(top_hbm, row.at[pl.ds(0, nb)])
        ]
        start, wait = chunks(
            c_sem, 0,
            [t_part(t_hbm, t_ref, local, nsucc), in_part(acc_hbm, acc_in), in_part(anc_hbm, anc)],
        )
        put, put_wait = chunks(
            c_sem, 3,
            [in_part(val, val_out), in_part(inv, inv_out), in_part(r, r_out)],
        )
        start_all(start)
        slot_acc[...] = jnp.zeros_like(slot_acc)
        for i in range(slots):
            w, top = weigh(got[i])
            wr[i] = w
            topr[i : i + 1] = top
        for c in early:
            c.wait()
        row[nb:nl] = topr[...]

        def one(b):
            top_all, a = remote_terms(
                b, info, lambda k: t_ref[b, k], wr, topr, peak_in[pl.ds(b, 1)], acc_in[b]
            )
            row[pl.ds(nl + b, 1)] = top_all
            live = b < info[2]
            v = new_values(top_all + jnp.log(a), b, cst)
            val[b] = jnp.where(live, v.astype(F32), 0.0).astype(BF16)
            share = jnp.where(live, 1.0 / a, 0.0)
            inv[b] = share
            r[b] = (anc[b].astype(F32) * share).astype(BF16)

        in_units(nb, one, wait)
        start_all(put)
        put_row = cps.add(row, row_out)

        def two(b):
            add_flows(b, r[b], info, lambda k: t_ref[b, k], local, nsucc, row, slot_acc, nb)

        in_units(nb, two)
        sent[...] = slot_acc[...].astype(BF16)
        for i in range(slots):
            invl[i] = inv[info[at_listed + i]]
        put_row.wait()
        wait_all(put_wait)

    last = call(
        last_body, [SMEM, VMEM, ANY, ANY, ANY, ANY, ANY, ANY],
        [
            (ANY, (nb, s, d), BF16), (ANY, (nb, s, d), F32), (ANY, (nb, s, d), BF16),
            (ANY, (rows, d), F32), (VMEM, (slots, s, d), BF16), (VMEM, (slots, s, d), F32),
        ],
        [
            const_spec(), pltpu.VMEM((nb, REMOTE, s, s), BF16),
            pltpu.VMEM((nb, s, d), F32), pltpu.VMEM((nb, d), F32), pltpu.VMEM((rows, d), F32),
            pltpu.VMEM((nb, s, d), BF16), pltpu.VMEM((nb, s, d), BF16),
            pltpu.VMEM((nb, s, d), F32), pltpu.VMEM((nb, s, d), BF16),
            pltpu.VMEM((slots, s, d), BF16), pltpu.VMEM((slots, d), F32),
            pltpu.VMEM((slots, s, d), F32),
            sems(4), pltpu.SemaphoreType.DMA((6, turns)),
        ],
        nb * 2 * REMOTE * pair, 14 << 20, "last",
    )

    def make_spread(first, final):
        ks = local if final else nsucc

        def body(*refs):
            refs = list(refs)
            info = refs.pop(0)
            r_listed = None if first else refs.pop(0)
            row_hbm, t_hbm, r_hbm, w_hbm = refs[:4]
            refs = refs[4:]
            inv_hbm = None if final else refs.pop(0)
            total_hbm = None if first else refs.pop(0)
            if final:
                vis_out, totl = refs[:2]
                refs = refs[2:]
            else:
                total_out, r_out, ownl, part = refs[:4]
                refs = refs[4:]
            row, t_ref, r_in, w2, total, own, sem, c_sem = refs[:8]
            refs = refs[8:]
            if final:
                vis = refs.pop(0)
            else:
                inv, r_next = refs
            get_row = pltpu.make_async_copy(row_hbm, row, sem.at[0])
            get_row.start()
            start, wait = chunks(c_sem, 0, [t_part(t_hbm, t_ref, 0, ks)])
            r_start, r_wait = chunks(c_sem, 1, [in_part(r_hbm, r_in)])
            later = [in_part(w_hbm, w2)]
            if not final:
                later.append(in_part(inv_hbm, inv))
            if not first:
                later.append(in_part(total_hbm, total))
            late_start, late_wait = chunks(c_sem, 2, later)
            if final:
                out_parts = [in_part(vis, vis_out)]
            else:
                out_parts = [in_part(own if first else total, total_out), in_part(r_next, r_out)]
            put, put_wait = chunks(c_sem, 5, out_parts)
            start_all(r_start)
            start_all(start)
            start_all(late_start)
            own[...] = jnp.zeros_like(own)
            wait_all(r_wait)
            if not first:
                for i in range(slots):
                    @pl.when(info[at_lead + i] == 1)
                    def _(i=i):
                        r_in[info[at_listed + i]] = r_listed[i]
            get_row.wait()

            def one(b):
                add_flows(b, r_in[b], info, lambda k: t_ref[b, k], 0, local, row, own, 0)

            in_units(nb, one, wait)
            if not final:
                part[...] = jnp.zeros_like(part)

            def before(g):
                late_wait(g)

                @pl.when(g > 0)
                def _():
                    put(g - 1)

            def two(b):
                if final:
                    sums = total[b] + own[b]
                    own[b] = sums
                    mass = jnp.where(b < info[2], w2[b].astype(F32) * sums, 0.0)
                    vis[b] = mass.astype(BF16)
                    return
                free = lax.convert_element_type(info[at_free + b], F32)
                r = (w2[b].astype(F32) * own[b] * (inv[b] * free)).astype(BF16)
                r_next[b] = r
                if not first:
                    total[b] = total[b] + own[b]
                add_flows(b, r, info, lambda k: t_ref[b, local + k], local, nsucc, row, part, nb)

            in_units(nb, two, before)
            put(turns - 1)
            for i in range(slots):
                if final:
                    totl[i] = own[info[at_listed + i]]
                else:
                    ownl[i] = own[info[at_listed + i]]
            wait_all(put_wait)

        if final:
            outs = [(ANY, (nb, s, d), BF16), (VMEM, (slots, s, d), F32)]
        else:
            outs = [
                (ANY, (nb, s, d), F32), (ANY, (nb, s, d), BF16),
                (VMEM, (slots, s, d), F32), (VMEM, (slots, s, d), F32),
            ]
        ins = [SMEM] + ([] if first else [VMEM]) + [ANY] * 4
        ins += ([] if final else [ANY]) + ([] if first else [ANY])
        scratch = [
            pltpu.VMEM((rows, d), F32), pltpu.VMEM((nb, ks, s, s), BF16),
            pltpu.VMEM((nb, s, d), BF16), pltpu.VMEM((nb, s, d), BF16),
            pltpu.VMEM((nb, s, d), F32), pltpu.VMEM((nb, s, d), F32),
            sems(1), pltpu.SemaphoreType.DMA((7, turns)),
        ]
        if final:
            scratch.append(pltpu.VMEM((nb, s, d), BF16))
        else:
            scratch += [pltpu.VMEM((nb, s, d), F32), pltpu.VMEM((nb, s, d), BF16)]
        return call(body, ins, outs, scratch, nb * ks * pair, 14 << 20, "spread")

    def make_join(first):
        def body(*refs):
            refs = list(refs)
            info, got, ownl, invl, wl, part, row_hbm, t_hbm = refs[:8]
            refs = refs[8:]
            back_in = None if first else refs.pop(0)
            sent, r_out, back, row, t_ref, sem, t_sem = refs

            def cp(i):
                return pltpu.make_async_copy(
                    t_hbm.at[info[at_listed + i], pl.ds(local, REMOTE)], t_ref.at[i], t_sem.at[i]
                )

            get_row = pltpu.make_async_copy(row_hbm, row, sem.at[0])
            get_row.start()
            for i in range(slots):
                cp(i).start()
            add_returned(info, got, back)
            get_row.wait()
            for i in range(slots):
                cp(i).wait()
            acc = part

            def one(i):
                b = info[at_listed + i]
                here = back[i]
                leads = lax.convert_element_type(info[at_lead + i], F32)
                mass = wl[i].astype(F32) * (ownl[i] + here)
                r_out[i] = (mass * (invl[i] * leads)).astype(BF16)
                if not first:
                    back[i] = back_in[i] + here

            in_units(slots, one)
            total = [None] * slots
            del total

            def two(i):
                b = info[at_listed + i]
                add_flows(b, r_out[i], info, lambda k: t_ref[i, k], local, nsucc, row, acc, nb)

            in_units(slots, two)
            sent[...] = acc[...].astype(BF16)

        def wrapped(*refs):
            refs = list(refs)
            scratch = refs.pop()
            scratch[...] = refs[5][...]
            refs[5] = scratch
            body(*refs)

        ins = [SMEM, VMEM, VMEM, VMEM, VMEM, VMEM, ANY, ANY] + ([] if first else [VMEM])
        return call(
            wrapped, ins,
            [
                (VMEM, (slots, s, d), BF16), (VMEM, (slots, s, d), BF16), (VMEM, (slots, s, d), F32),
            ],
            [
                pltpu.VMEM((rows, d), F32), pltpu.VMEM((slots, REMOTE, s, s), BF16),
                sems(1), sems(slots), pltpu.VMEM((slots, s, d), F32),
            ],
            slots * REMOTE * pair, 4 << 20, "join",
        )

    def add_returned(info, got, back):
        back[...] = jnp.zeros_like(back)
        for i in range(slots):
            j = info[at_owner + i]
            back[j] = back[j] + got[i].astype(F32)

    def close_body(info, got, totl, wl, back_in, vis_in, vis_out, back, stage, sem):
        del vis_in
        back[...] = back_in[...]
        for i in range(slots):
            j = info[at_owner + i]
            back[j] = back[j] + got[i].astype(F32)
        for i in range(slots):
            stage[i] = (wl[i].astype(F32) * (totl[i] + back[i])).astype(BF16)

        def cp(i):
            return pltpu.make_async_copy(stage.at[i], vis_out.at[info[at_listed + i]], sem.at[i])

        for i in range(slots):
            @pl.when(info[at_lead + i] == 1)
            def _(i=i):
                cp(i).start()

        for i in range(slots):
            @pl.when(info[at_lead + i] == 1)
            def _(i=i):
                cp(i).wait()

    close = pl.pallas_call(
        close_body,
        out_shape=sds((nb, s, d), BF16),
        in_specs=[SMEM] + [VMEM] * 4 + [ANY],
        out_specs=ANY,
        scratch_shapes=[
            pltpu.VMEM((slots, s, d), F32), pltpu.VMEM((slots, s, d), BF16), sems(slots),
        ],
        input_output_aliases={5: 0},
        compiler_params=pltpu.CompilerParams(vmem_limit_bytes=GRANT),
        cost_estimate=pl.CostEstimate(flops=blk, bytes_accessed=2 << 20, transcendentals=0),
        name="close",
    )

    return dict(
        pack=pack, begin=begin, sweep_first=sweep_first, listed_next=listed_next,
        sweep_next=sweep_next, last=last, spread=make_spread, join=make_join, close=close,
    )


class WeightView:
    def __init__(self, ref, rows):
        self.ref, self.rows = ref, rows

    def __getitem__(self, e):
        return self.ref[e, 0 : self.rows]


def swap(parcels, axis):
    return lax.all_to_all(parcels, axis, split_axis=0, concat_axis=0, tiled=True)


def total_over(x, axis):
    n = lax.axis_size(axis)
    return jnp.sum(swap(jnp.broadcast_to(x[None], (n,) + x.shape), axis), axis=0)


def on_device(
    coarse, region_map, features, reward_weights, transitions, successors,
    part_sizes, outgoing_block_list, destinations, anchors,
):
    nb, nsucc, s, _ = transitions.shape
    rdev, d = coarse.shape
    n_dom = lax.axis_size("dom")
    per_peer = outgoing_block_list.shape[2]
    slots = n_dom * per_peer
    feat = features.shape[0]
    grp_first = lax.axis_index("grp") * n_dom
    linear = grp_first + lax.axis_index("dom")
    ks = make_kernels(nb, nsucc, s, d, slots, n_dom, rdev)

    listed = outgoing_block_list.reshape(slots)
    same = listed[:, None] == listed[None, :]
    owner = jnp.argmax(same, axis=1).astype(I32)
    lead = (owner == jnp.arange(slots, dtype=I32)).astype(I32)
    free = 1 - jnp.any(listed[None, :] == jnp.arange(nb, dtype=I32)[:, None], axis=1).astype(I32)
    base = linear * (nb * s)
    info = jnp.concatenate(
        [
            jnp.stack([base, grp_first, part_sizes[0], jnp.int32(0)]).astype(I32),
            successors.reshape(nb * nsucc), listed, lead, owner, free,
        ]
    )
    regions = region_map.reshape(nb, s)
    (parcels,) = ks["pack"](info, coarse, regions)
    rec = swap(parcels, "dom")

    rewards = jnp.dot(
        reward_weights[None, :], features.astype(F32), precision=lax.Precision.HIGHEST
    )[0]
    cst = jnp.concatenate(
        [
            jnp.pad(rewards.reshape(nb, s).T, ((0, 0), (0, 128 - nb))),
            jnp.broadcast_to((destinations - base).astype(F32)[None, :], (8, d)),
        ],
        axis=0,
    )

    w0, top0, sent = ks["begin"](info, rec, regions, cst, transitions)
    got = swap(sent, "dom")
    acc, peak, accl = ks["sweep_first"](info, cst, transitions, w0, top0)
    sent, wr = ks["listed_next"](info, got, accl, cst, transitions)
    got = swap(sent, "dom")
    w2, top2, acc, peak, wl = ks["sweep_next"](info, wr, cst, transitions, acc, peak)
    values, inv, r, row, sent, invl = ks["last"](
        info, got, cst, transitions, acc, peak, top2, anchors.reshape(nb, s, d)
    )
    got = swap(sent, "dom")
    total, r, ownl, part = ks["spread"](True, False)(info, row, transitions, r, w2, inv)
    sent, rl, back = ks["join"](True)(info, got, ownl, invl, wl, part, row, transitions)
    got = swap(sent, "dom")
    total, r, ownl, part = ks["spread"](False, False)(
        info, rl, row, transitions, r, w2, inv, total
    )
    sent, rl, back = ks["join"](False)(info, got, ownl, invl, wl, part, row, transitions, back)
    got = swap(sent, "dom")
    visits, totl = ks["spread"](False, True)(info, rl, row, transitions, r, w2, total)
    visits = ks["close"](info, got, totl, wl, back, visits)

    values = values.reshape(nb * s, d)
    visits = visits.reshape(nb * s, d)
    live_rows = (jnp.arange(nb * s, dtype=I32) // s < part_sizes[0])[:, None]
    mass = jnp.sum(jnp.where(live_rows, anchors.astype(F32), 0.0), axis=0, keepdims=True)
    part_counts = jnp.dot(features, visits, preferred_element_type=F32)
    sums = jnp.concatenate([part_counts, jnp.broadcast_to(mass, (8, d))], axis=0)
    sums = total_over(total_over(sums, "dom"), "grp")
    return values, visits, sums[:feat] / sums[feat : feat + 1]


def solution(mesh):
    every = ("grp", "dom")
    return jax.shard_map(
        on_device,
        mesh=mesh,
        in_specs=(
            P(every, None), P(every), P(None, every), P(), P(every, None, None, None),
            P(every, None), P(every), P(every, None, None), P(), P(every, None),
        ),
        out_specs=(P(every, None), P(every, None), P()),
        check_vma=False,
    )
```
